32 devices in a mesh: ep: 8 (over z, y), tp: 4 (over x, core).
Axes of the slice: x: 2, y: 2, z: 4, core: 2. Of those that a mesh axis runs over, the one named last changes fastest.
Arguments:
- tokens: bfloat16 [1024, 4096], P('ep', 'tp'), may hold values from -6 to 6
- out_grad: bfloat16 [1024, 4096], P('ep', 'tp'), may hold values from -6 to 6
- expert_ids: int32 [1024, 4], P('ep'), may hold values from 0 to 7, all different within a row; in each aligned block of 128 rows (0 to 127, 128 to 255, ...) at most 72 rows name the same one
- route_probs: float32 [1024, 4], P('ep'), may hold values from 0.05 to 0.5
- w_gate: bfloat16 [8, 4096, 768], P('ep', 'tp'), may hold values from -0.09375 to 0.09375
- w_up: bfloat16 [8, 4096, 768], P('ep', 'tp'), may hold values from -0.09375 to 0.09375
- w_down: bfloat16 [8, 768, 4096], P('ep', None, 'tp'), may hold values from -0.21875 to 0.21875
Outputs:
- grad_tokens: bfloat16 [1024, 4096], P('ep', 'tp')
- fisher_gate: bfloat16 [8, 4096, 768], P('ep', 'tp')
- fisher_up: bfloat16 [8, 4096, 768], P('ep', 'tp')
- fisher_down: bfloat16 [8, 768, 4096], P('ep', None, 'tp')
The draws below stay inside these ranges and needn't reach their ends.
Inputs may be any that keep to these rules, and one draw needn't show every extreme that they name: `expert_ids`: each token names 4 different experts; among the tokens of one index of ep no expert is named by more than 72 tokens, a bound that some block reaches.
All inputs are finite; a program needn't handle non-finite values.
Results may differ from the reference program's by a relative error of at most 0.03.
Values may be sent and summed in bfloat16 or wider, within the bound.
A program may use at most 128 MiB of HBM per device.

```python
import math
import jax
import jax.numpy as jnp
import numpy as np
from jax import lax

D = 4096
FF = 768
TOK_DEV = 128
TOKENS = 1024
EXPERTS = 8
TOPK = 4
CAP = 72
N_EP = 8
N_TP = 4


def block_levels(stream_key, extent, shards, low, high):
    loudness, own = 1.0, jax.random.fold_in(stream_key, 6)
    for axis_at, blocks in shards:
        draws = jnp.exp(jax.random.uniform(jax.random.fold_in(own, axis_at), (blocks,), jnp.float32, low / len(shards), high / len(shards)))
        loudness = loudness * jnp.repeat(draws, extent[axis_at] // blocks).reshape([-1 if axis == axis_at else 1 for axis in range(len(extent))])
    return loudness


def routed_block(rng, own, number, rows, count, top, bound, skew):
    order = jax.random.permutation(rng, count)
    packed, common = load_shares(count, rows * top, bound, skew, True), load_shares(count, rows * top, bound, skew, False)
    places = jnp.arange(count)

    def named(lengths, rotation):
        used = int((lengths > 0).sum())
        fixed = max(1, used // 4)
        moved = fixed + (places - fixed + rotation * (used - fixed)) % max(1, count - fixed)
        return jnp.zeros((count,), jnp.int32).at[order[jnp.where(places < fixed, places, moved)]].set(jnp.asarray(lengths, jnp.int32))

    lengths = jnp.where(number % 4 == 0, named(packed, number // 4), named(common, number - number // 4 - 1))
    mixed = jax.random.permutation(jax.random.fold_in(own, 3), count)
    giver, sink = mixed[0:count // 2 * 2:2], mixed[1:count // 2 * 2:2]
    room = jnp.minimum(lengths[giver] - 1, bound - lengths[sink]) // 2
    room = jnp.where((giver == order[0]) | (sink == order[0]) | (lengths[sink] == 0), 0, jnp.maximum(room, 0))
    moved = jax.random.randint(jax.random.fold_in(own, 4), (count // 2,), 0, 1 << 20) % (room + 1)
    lengths = lengths.at[giver].add(-moved).at[sink].add(moved)
    labels = jnp.searchsorted(jnp.cumsum(lengths), jnp.arange(rows * top), side="right").astype(jnp.int32)
    grid = labels.reshape(top, rows).T
    grid = grid[jax.random.permutation(jax.random.fold_in(own, 1), rows)]
    rotation = jax.random.randint(jax.random.fold_in(own, 2), (rows, 1), 0, top)
    return jnp.take_along_axis(grid, (jnp.arange(top)[None, :] + rotation) % top, axis=1)


def load_shares(number_of, total, reach, slope, full):
    loads = [(1 << 20) // math.isqrt(standing ** slope) + 1 for standing in range(1, number_of + 1)]
    largest = reach if full else min(reach, max(-(-total // number_of), total * loads[0] // sum(loads)))
    least = 1 if total - largest >= number_of - 1 else 0
    given, surplus = [largest] + [least] * (number_of - 1), total - largest - least * (number_of - 1)
    while surplus > 0:
        free = [i for i in range(1, number_of) if given[i] < largest] or [i for i in range(1, number_of) if given[i] < reach]
        whole, left = sum([loads[i] for i in free]), surplus
        for i in free:
            more = min(reach - given[i], max(1, left * loads[i] // whole), surplus)
            given[i] = given[i] + more
            surplus = surplus - more
    return np.array(given)


def normal_values(key, extent, scale, bound, cuts=(), held_as=jnp.bfloat16):
    values = jax.random.normal(key, extent, jnp.float32) * scale
    if len(cuts) > 0:
        values = block_levels(key, extent, cuts, -0.22, 0.18) * values
    return jnp.clip(values, min=-bound, max=bound).astype(held_as)


def setup_inputs(seed: int = 0) -> dict:
    key_list = jax.random.split(jax.random.key(seed), 8)
    tokens = normal_values(key_list[0], (TOKENS, D), 1.0, 6.0, ((0, 8), (1, 4)))
    out_grad = normal_values(key_list[1], (TOKENS, D), 1.0, 6.0, ((0, 8), (1, 4)))
    expert_ids_keys = jax.random.split(jax.random.fold_in(key_list[2], 1), TOKENS // TOK_DEV)
    expert_ids_turns = jax.random.permutation(jax.random.fold_in(key_list[2], 3), TOKENS // TOK_DEV)
    expert_ids = jax.vmap(lambda own, number: routed_block(jax.random.fold_in(key_list[2], 2), own, number, TOK_DEV, EXPERTS, TOPK, CAP, 2))(expert_ids_keys, expert_ids_turns).reshape((TOKENS, TOPK))
    route_probs = jnp.clip(jnp.exp(math.log(0.5) - 2.3025851 * jax.random.uniform(key_list[3], (TOKENS, TOPK), jnp.float32) ** block_levels(key_list[3], (TOKENS, TOPK), ((0, 8),), -0.2, 0.2)), 0.05, 0.5)
    w_gate = normal_values(key_list[4], (EXPERTS, D, FF), D ** -0.5, 0.09375, ((0, 8), (1, 4)))
    w_up = normal_values(key_list[5], (EXPERTS, D, FF), D ** -0.5, 0.09375, ((0, 8), (1, 4)))
    w_down = normal_values(key_list[6], (EXPERTS, FF, D), FF ** -0.5, 0.21875, ((0, 8), (2, 4)))
    return dict(tokens=tokens, out_grad=out_grad, expert_ids=expert_ids, route_probs=route_probs, w_gate=w_gate, w_up=w_up, w_down=w_down)


def reference(tokens, out_grad, expert_ids, route_probs, w_gate, w_up, w_down):
    assigns = TOK_DEV * TOPK
    quarter = D // N_TP
    blocks = expert_ids.reshape(N_EP, assigns).astype(jnp.int32)
    onehot = (blocks[:, :, None] == jnp.arange(EXPERTS, dtype=jnp.int32)[None, None, :]).astype(jnp.int32)
    ranks = jnp.sum((jnp.cumsum(onehot, 1) - onehot) * onehot, 2).astype(jnp.int32)
    slots = (blocks * CAP + ranks).astype(jnp.int32)
    global_ids = (jnp.arange(N_EP, dtype=jnp.int32) * assigns)[:, None] + jnp.arange(assigns, dtype=jnp.int32)[None, :]

    def fill_row(slot_row, id_row):
        return jnp.full((EXPERTS * CAP,), TOKENS * TOPK, jnp.int32).at[slot_row].set(id_row)

    table = jax.vmap(fill_row)(slots, global_ids)
    table = table.reshape(N_EP, EXPERTS, CAP).transpose(1, 0, 2).reshape(EXPERTS, N_EP * CAP)
    padded_x = jnp.concatenate([tokens, jnp.zeros((1, D), tokens.dtype)], 0)
    padded_dy = jnp.concatenate([out_grad, jnp.zeros((1, D), out_grad.dtype)], 0)
    padded_p = jnp.concatenate([route_probs.reshape(-1), jnp.zeros((1,), jnp.float32)], 0)
    scale = 1.0 / TOK_DEV

    def expert_step(accum, inputs):
        e_table, gate_mat, up_mat, down_mat = inputs
        token_of = (e_table // TOPK).astype(jnp.int32)
        x_rows = padded_x[token_of]
        dy_rows = (padded_dy[token_of].astype(jnp.float32) * padded_p[e_table][:, None]).astype(jnp.bfloat16)
        x_quart = x_rows.astype(jnp.float32).reshape(-1, N_TP, quarter)
        dy_quart = dy_rows.astype(jnp.float32).reshape(-1, N_TP, quarter)
        gate = jnp.sum(jnp.einsum('sqd,qdf->qsf', x_quart, gate_mat.astype(jnp.float32).reshape(N_TP, quarter, FF)).astype(jnp.bfloat16).astype(jnp.float32), 0)
        up = jnp.sum(jnp.einsum('sqd,qdf->qsf', x_quart, up_mat.astype(jnp.float32).reshape(N_TP, quarter, FF)).astype(jnp.bfloat16).astype(jnp.float32), 0)
        dact = jnp.sum(jnp.einsum('sqd,fqd->qsf', dy_quart, down_mat.astype(jnp.float32).reshape(FF, N_TP, quarter)).astype(jnp.bfloat16).astype(jnp.float32), 0)
        sig = jax.nn.sigmoid(gate)
        act = (gate * sig * up).astype(jnp.bfloat16)
        dgate = (dact * up * sig * (1.0 + gate * (1.0 - sig))).astype(jnp.bfloat16)
        dup = (dact * gate * sig).astype(jnp.bfloat16)
        dx_rows = (jnp.dot(dgate, gate_mat.T, preferred_element_type=jnp.float32) + jnp.dot(dup, up_mat.T, preferred_element_type=jnp.float32)).astype(jnp.bfloat16)
        accum = accum.at[token_of].add(dx_rows.astype(jnp.float32))
        x_sq = jnp.square(x_rows.astype(jnp.float32)).astype(jnp.bfloat16)
        act_sq = jnp.square(act.astype(jnp.float32)).astype(jnp.bfloat16)
        dg_sq = jnp.square(dgate.astype(jnp.float32)).astype(jnp.bfloat16)
        du_sq = jnp.square(dup.astype(jnp.float32)).astype(jnp.bfloat16)
        dy_sq = jnp.square(dy_rows.astype(jnp.float32)).astype(jnp.bfloat16)
        fish_gate = (jnp.dot(x_sq.T, dg_sq, preferred_element_type=jnp.float32) * scale).astype(jnp.bfloat16)
        fish_up = (jnp.dot(x_sq.T, du_sq, preferred_element_type=jnp.float32) * scale).astype(jnp.bfloat16)
        fish_down = (jnp.dot(act_sq.T, dy_sq, preferred_element_type=jnp.float32) * scale).astype(jnp.bfloat16)
        return accum, (fish_gate, fish_up, fish_down)

    start = jnp.zeros((TOKENS + 1, D), jnp.float32)
    accum, outs = lax.scan(expert_step, start, (table, w_gate, w_up, w_down))
    grad_tokens = accum[:TOKENS].astype(jnp.bfloat16)
    return grad_tokens, outs[0], outs[1], outs[2]
```

```python
import functools

import jax
import jax.numpy as jnp
from jax import lax
from jax.experimental import pallas as pl
from jax.experimental.pallas import tpu as pltpu
from jax.sharding import PartitionSpec as P


def contract_rows(left, right):
    return lax.dot_general(
        left, right, (((0,), (0,)), ((), ())), preferred_element_type=jnp.float32
    )


def contract_cols(left, right):
    return lax.dot_general(
        left, right, (((1,), (1,)), ((), ())), preferred_element_type=jnp.float32
    )


def swiglu_back(gate, up, dact):
    sig = jax.nn.sigmoid(gate)
    act = (gate * sig * up).astype(jnp.bfloat16)
    dgate = (dact * up * sig * (1.0 + gate * (1.0 - sig))).astype(jnp.bfloat16)
    dup = (dact * gate * sig).astype(jnp.bfloat16)
    return (act, dgate, dup)


def squared(values):
    return jnp.square(values.astype(jnp.float32)).astype(jnp.bfloat16)


def on_device(tokens, out_grad, expert_ids, route_probs, w_gate, w_up, w_down):
    tok_rows = tokens.shape[0]
    width_part = tokens.shape[1]
    top_count = expert_ids.shape[1]
    experts = lax.axis_size("ep")
    capacity = tok_rows * top_count * 9 // (8 * experts)
    assigns = tok_rows * top_count
    flat_ids = expert_ids.reshape(-1)
    onehot = (flat_ids[:, None] == jnp.arange(experts, dtype=jnp.int32)[None, :]).astype(jnp.int32)
    ranks = jnp.sum((jnp.cumsum(onehot, 0) - onehot) * onehot, 1)
    slot_index = flat_ids * capacity + ranks
    table = (
        jnp.full((experts * capacity,), assigns, jnp.int32)
        .at[slot_index]
        .set(jnp.arange(assigns, dtype=jnp.int32))
    )
    token_of = table // top_count
    padded_x = jnp.concatenate([tokens, jnp.zeros((1, width_part), tokens.dtype)], 0)
    padded_dy = jnp.concatenate([out_grad, jnp.zeros((1, width_part), out_grad.dtype)], 0)
    padded_p = jnp.concatenate([route_probs.reshape(-1), jnp.zeros((1,), jnp.float32)], 0)
    send_x = padded_x[token_of].reshape(experts, capacity, width_part)
    send_dy = (padded_dy[token_of].astype(jnp.float32) * padded_p[table][:, None]).astype(
        jnp.bfloat16
    )
    send_dy = send_dy.reshape(experts, capacity, width_part)
    gate_mat = w_gate[0]
    up_mat = w_up[0]
    down_mat = w_down[0]
    recv_x, recv_dy = (
        lax.all_to_all(send_x, "ep", split_axis=0, concat_axis=0, tiled=True),
        lax.all_to_all(send_dy, "ep", split_axis=0, concat_axis=0, tiled=True),
    )
    recv_x = recv_x.reshape(-1, width_part)
    recv_dy = recv_dy.reshape(-1, width_part)
    gate_part = jnp.dot(recv_x, gate_mat, preferred_element_type=jnp.float32)
    up_part = jnp.dot(recv_x, up_mat, preferred_element_type=jnp.float32)
    dact_part = contract_cols(recv_dy, down_mat)
    gate, up, dact = (
        lax.psum(gate_part.astype(jnp.bfloat16), "tp").astype(jnp.float32),
        lax.psum(up_part.astype(jnp.bfloat16), "tp").astype(jnp.float32),
        lax.psum(dact_part.astype(jnp.bfloat16), "tp").astype(jnp.float32),
    )
    act, dgate, dup = swiglu_back(gate, up, dact)
    dx_rows = (contract_cols(dgate, gate_mat) + contract_cols(dup, up_mat)).astype(jnp.bfloat16)
    returned = lax.all_to_all(
        dx_rows.reshape(experts, capacity, width_part),
        "ep",
        split_axis=0,
        concat_axis=0,
        tiled=True,
    )
    scale = 1.0 / tok_rows
    x_sq = squared(recv_x)
    fisher_gate = (contract_rows(x_sq, squared(dgate)) * scale).astype(jnp.bfloat16)[None]
    fisher_up = (contract_rows(x_sq, squared(dup)) * scale).astype(jnp.bfloat16)[None]
    fisher_down = (contract_rows(squared(act), squared(recv_dy)) * scale).astype(jnp.bfloat16)[None]
    pulled = returned.reshape(experts * capacity, width_part)[slot_index].astype(jnp.float32)
    grad_tokens = jnp.sum(pulled.reshape(tok_rows, top_count, width_part), 1).astype(jnp.bfloat16)
    return (grad_tokens, fisher_gate, fisher_up, fisher_down)


MESH = pl.DeviceIdType.MESH
F32 = jnp.float32
BF16 = jnp.bfloat16
ROW_TILE = 8
LANES = 128
VMEM_BYTES = 44 * 1024 * 1024
OPENING = """X00 X01 M00"""
INNER = """A10 X10 X20 M01 S00 S01 M10 S10 A11 X11 X21 M20 S20 V0 A20 X30 M11 S11 D0
M21 S21 A21 X31 V1 M30 S30 D1 R1 V2 M31 S31 D2 R2 R0 A30 A31 V3 D3 R3"""
OUTER = """A10 X10 M01 S00 S01 A11 X11 M10 S10 A20 X20 M11 V0 S11 A21 X21 M20 S20 V1 D0 D1 R1
A30 X30 M21 S21 A31 X31 M30 S30 V2 D2 R2 R0 M31 S31 V3 D3 R3"""


def flipped(index, mask):
    out, bit = index, 1
    while bit <= mask:
        if mask & bit:
            out = out + bit * (1 - 2 * ((index // bit) % 2))
        bit *= 2
    return out


def slot_rows(tok_rows, top_count, experts):
    capacity = tok_rows * top_count * 9 // (8 * experts)
    return -(-capacity // ROW_TILE) * ROW_TILE


def visiting_order(row):
    low = 1 - row // 2
    return (
        row,
        row - 1 + 2 * low,
        low * (2 - 2 * row) + (1 - low) * (7 - 2 * row),
        3 * low,
    )


def fused_kernel(
    n_ep, n_tp, rows,
    tok_hbm, og_hbm, ids_hbm, rp_hbm, wg_hbm, wu_hbm, wd_hbm,
    fg, fu, fd, ret, onehot,
    wg, wu, wd, ids, rp, pe, rank, peb, tb, sx, rx, pb, rb, sb, rb2, af, dxs, tsx, tsa, dsq, gsq, usq,
    w_sem, l_sem, pes_sem, per_sem, ts_sem, tr_sem, xs_sem, xr_sem,
    ps_sem, pr_sem, qs_sem, qr_sem, as_sem, ar_sem, ds_sem, dr_sem,
):
    e = lax.axis_index("ep")
    q = lax.axis_index("tp")
    row, mate = e // 2, flipped(e, 1)
    core = q % 2
    near, far = flipped(q, 1), flipped(q, 2)
    tok_rows, width = tok_hbm.shape
    ff = wg.shape[1]
    pair = 2 * rows
    chunks = n_ep // 2
    scale = 1.0 / tok_rows
    order = visiting_order(row)

    blocks = [
        pltpu.make_async_copy(hbm, tb.at[row, i], l_sem.at[i])
        for i, hbm in enumerate((tok_hbm, og_hbm))
    ]
    routes = [
        pltpu.make_async_copy(hbm, vmem, l_sem.at[2 + i])
        for i, (hbm, vmem) in enumerate(((ids_hbm, ids), (rp_hbm, rp)))
    ]
    loads = [
        pltpu.make_async_copy(hbm.at[0], vmem, w_sem.at[i])
        for i, (hbm, vmem) in enumerate(((wg_hbm, wg), (wu_hbm, wu), (wd_hbm, wd)))
    ]
    for copy in routes + blocks + loads:
        copy.start()

    barrier = pltpu.get_barrier_semaphore()
    for k in range(1, n_ep):
        pl.semaphore_signal(barrier, inc=1, device_id=(flipped(e, k), q), device_id_type=MESH)
    for j in (1, 2):
        pl.semaphore_signal(barrier, inc=1, device_id=(e, flipped(q, j)), device_id_type=MESH)
    before = (
        lax.broadcasted_iota(jnp.int32, (tok_rows, tok_rows), 0)
        < lax.broadcasted_iota(jnp.int32, (tok_rows, tok_rows), 1)
    ).astype(BF16)
    slot_iota = lax.broadcasted_iota(jnp.int32, (rows, tok_rows), 0)
    for copy in routes:
        copy.wait()
    names = lax.broadcasted_iota(jnp.int32, (n_ep, tok_rows), 0)
    probs = jnp.zeros((n_ep, tok_rows), F32)
    for k in range(ids.shape[0]):
        probs = probs + jnp.where(ids[pl.ds(k, 1), :] == names, rp[pl.ds(k, 1), :], 0.0)
    pe[...] = probs
    for copy in blocks:
        copy.wait()
    pl.semaphore_wait(barrier, n_ep + 1)

    def remote(src, dst, send_sem, recv_sem, device):
        return pltpu.make_async_remote_copy(
            src_ref=src,
            dst_ref=dst,
            send_sem=send_sem,
            recv_sem=recv_sem,
            device_id=device,
            device_id_type=MESH,
        )

    def block(k):
        return pl.ds(k * rows, rows)

    def span(c):
        return pl.ds(c * pair, pair)

    def hop(direction, distance, i):
        step = 1 - 2 * direction
        held = tb.at[row - step * distance, i]
        return remote(
            held,
            held,
            ts_sem.at[direction, distance, i],
            tr_sem.at[direction, distance, i],
            (e + 2 * step, q),
        )

    def sends(direction, distance):
        if direction == 0:
            return (row >= distance) & (row < chunks - 1)
        return (row + distance < chunks) & (row > 0)

    def holds(direction, distance):
        if direction == 0:
            return row >= distance
        return row + distance < chunks

    def landed(direction, distance, i):
        held = tb.at[row - (1 - 2 * direction) * distance, i]
        return remote(
            held,
            held,
            ts_sem.at[direction, distance - 1, i],
            tr_sem.at[direction, distance - 1, i],
            (mate, q),
        )

    def arrive(distance, i):
        for direction in range(2):
            if distance:

                @pl.when(holds(direction, distance))
                def _():
                    landed(direction, distance, i).wait_recv()

            if distance < chunks - 1:

                @pl.when(sends(direction, distance))
                def _():
                    hop(direction, distance, i).start()

    def probs_copy(k, source):
        return remote(
            pe, peb.at[source], pes_sem.at[k], per_sem.at[source], (flipped(e, 2 * k), q)
        )

    def send_probs():
        for k in range(1, chunks):
            probs_copy(k, row).start()

    def x_copy(c, i):
        return remote(
            sx.at[i, block(c), :],
            rx.at[i, block(2 * c + 1), :],
            xs_sem.at[c, i],
            xr_sem.at[c, i],
            (mate, q),
        )

    def select(c, i):
        source = order[c]
        held = peb.at[source] if c else pe
        if i == 0:
            if c:
                probs_copy(1, source).wait_recv()
            mask = (held[...] > 0.0).astype(F32)
            ranks = jnp.dot(mask.astype(BF16), before, preferred_element_type=F32)
            rank[c] = jnp.where(mask > 0.0, ranks, -1.0).astype(jnp.int32)
        hots = [
            (slot_iota == rank[c, pl.ds(dest, 1), :]).astype(F32) for dest in (mate, e)
        ]
        rows_of = tb[source, i]
        for j, dest in enumerate((mate, e)):
            picked = jnp.dot(hots[j].astype(BF16), rows_of, preferred_element_type=F32)
            if i:
                picked = picked * jnp.sum(hots[j] * held[pl.ds(dest, 1), :], 1, keepdims=True)
            if j == 0:
                sx[i, block(c), :] = picked.astype(BF16)
                x_copy(c, i).start()
            else:
                rx[i, block(2 * c), :] = picked.astype(BF16)

    def part(index):
        return pl.ds(pl.multiple_of(index * rows, ROW_TILE), rows)

    groups = (pl.ds(0, 2), pl.ds(2, 1))

    def p_copy(c, i):
        return remote(
            pb.at[c, groups[i], part(1 - core), :],
            rb.at[c, groups[i]],
            ps_sem.at[c, i],
            pr_sem.at[c, i],
            (e, near),
        )

    def partials(c, i):
        x_copy(c, i).wait_recv()
        if i == 0:
            x = rx[0, span(c), :]
            if c == 0:
                loads[0].wait()
            pb[c, 0] = jnp.dot(x, wg[...], preferred_element_type=F32).astype(BF16)
            if c == 0:
                loads[1].wait()
            pb[c, 1] = jnp.dot(x, wu[...], preferred_element_type=F32).astype(BF16)
        else:
            if c == 0:
                loads[2].wait()
            pb[c, 2] = contract_cols(rx[1, span(c), :], wd[...]).astype(BF16)
        p_copy(c, i).start()

    def q_copy(c, i):
        return remote(
            sb.at[c, groups[i]], rb2.at[c, groups[i]], qs_sem.at[c, i], qr_sem.at[c, i], (e, far)
        )

    def pair_sum(c, i):
        p_copy(c, i).wait_recv()
        for n in ((0, 1), (2,))[i]:
            sb[c, n] = (pb[c, n, part(core), :].astype(F32) + rb[c, n].astype(F32)).astype(BF16)
        q_copy(c, i).start()

    products = (pl.ds(1, 2), pl.ds(0, 1))

    def a_copy(c, j, owner):
        held = af.at[products[j], part(2 * c + owner), :]
        return remote(held, held, as_sem.at[c, j], ar_sem.at[c, j], (e, near))

    def activate(c):
        for i in range(2):
            q_copy(c, i).wait_recv()
        gate, up, dact = [
            pb[c, n, part(core), :].astype(F32) + rb[c, n].astype(F32) + rb2[c, n].astype(F32)
            for n in range(3)
        ]
        for n, value in enumerate(swiglu_back(gate, up, dact)):
            af[n, part(2 * c + core), :] = value
        for j in range(2):
            a_copy(c, j, core).start()

    def input_grad(c):
        a_copy(c, 0, 1 - core).wait_recv()
        dx = contract_cols(af[1, span(c), :], wg[...]) + contract_cols(af[2, span(c), :], wu[...])
        dxs[span(c), :] = dx.astype(BF16)
        if c == 0:
            ret[part(e), :] = dxs[block(0), :]

    def d_copy(c, j):
        return remote(
            dxs.at[block(2 * c + j), :],
            ret.at[part(e), :],
            ds_sem.at[2 * c + j],
            dr_sem.at[e],
            (2 * order[c] + (e + j) % 2, q),
        )

    def give_back(c):
        for j in range(2):
            if c or j:
                d_copy(c, j).start()

    def transposed_squares(source, i, columns, out):
        @pl.loop(0, columns // LANES)
        def _(step):
            l = pl.ds(pl.multiple_of(step * LANES, LANES), LANES)
            out[l, :] = squared(source[i, :, l]).T

    def fisher(left, right, out):
        @pl.loop(0, left.shape[0] // LANES)
        def _(step):
            r = pl.ds(pl.multiple_of(step * LANES, LANES), LANES)
            sums = jnp.dot(left[r, :], right[...], preferred_element_type=F32)
            out[r, :] = (sums * scale).astype(BF16)

    stages = dict(
        A=arrive, X=select, M=partials, S=pair_sum, V=activate, D=input_grad, R=give_back
    )

    def run(names):
        for name in names.split():
            with jax.named_scope(name):
                stages[name[0]](*(int(digit) for digit in name[1:]))

    arrive(0, 0)
    send_probs()
    arrive(0, 1)
    run(OPENING)

    @pl.when((row > 0) & (row < chunks - 1))
    def _():
        run(INNER)

    @pl.when((row == 0) | (row == chunks - 1))
    def _():
        run(OUTER)

    last = chunks - 1
    with jax.named_scope("gsq"):
        for k in range(n_ep):
            onehot[block(k), :] = (slot_iota == rank[0, pl.ds(k, 1), :]).astype(F32).astype(BF16)
        gsq[...] = squared(af[1])
    with jax.named_scope("tsx"):
        transposed_squares(rx, 0, width, tsx)
    with jax.named_scope("fg"):
        fisher(tsx, gsq, fg)
    with jax.named_scope("usq"):
        usq[...] = squared(af[2])
    with jax.named_scope("fu"):
        fisher(tsx, usq, fu)
    with jax.named_scope("tsa"):
        for c in range(chunks):
            a_copy(c, 1, 1 - core).wait_recv()
        transposed_squares(af, 0, ff, tsa)
    with jax.named_scope("fd"):
        dsq[...] = squared(rx[1])
        fisher(tsa, dsq, fd)

    with jax.named_scope("retwait"):
        for k in range(1, n_ep):
            other = flipped(e, k)
            held = ret.at[part(other), :]
            remote(held, held, ds_sem.at[0], dr_sem.at[other], (other, q)).wait_recv()

    with jax.named_scope("sendwait"):
        for distance in range(chunks - 1):
            for direction in range(2):

                @pl.when(sends(direction, distance))
                def _():
                    for i in range(2):
                        hop(direction, distance, i).wait_send()

        for k in range(1, chunks):
            probs_copy(k, row).wait_send()
        for c in range(chunks):
            for i in range(2):
                for copy in (x_copy(c, i), p_copy(c, i), q_copy(c, i), a_copy(c, i, core)):
                    copy.wait_send()
                if c or i:
                    d_copy(c, i).wait_send()


def finish_kernel(fg, fu, fd, ret, onehot, grad_hbm, fg_hbm, fu_hbm, fd_hbm, grad, sem):
    copies = [
        pltpu.make_async_copy(vmem, hbm.at[0], sem.at[i])
        for i, (vmem, hbm) in enumerate(((fg, fg_hbm), (fu, fu_hbm), (fd, fd_hbm)))
    ]
    for copy in copies:
        copy.start()
    grad[...] = contract_rows(onehot[...], ret[...]).astype(BF16)
    copies.append(pltpu.make_async_copy(grad, grad_hbm, sem.at[3]))
    copies[3].start()
    for copy in copies:
        copy.wait()


def fused_on_device(n_ep, n_tp, tokens, out_grad, expert_ids, route_probs, w_gate, w_up, w_down):
    tok_rows, width = tokens.shape
    top_count = expert_ids.shape[1]
    ff = w_gate.shape[2]
    rows = slot_rows(tok_rows, top_count, n_ep)
    total, chunks = n_ep * rows, n_ep // 2
    hbm_spec = pl.BlockSpec(memory_space=pltpu.HBM)
    vmem_spec = pl.BlockSpec(memory_space=pltpu.VMEM)
    dma = pltpu.SemaphoreType.DMA
    *fishers, returned, onehot = pl.pallas_call(
        functools.partial(fused_kernel, n_ep, n_tp, rows),
        out_shape=(
            jax.ShapeDtypeStruct((width, ff), BF16),
            jax.ShapeDtypeStruct((width, ff), BF16),
            jax.ShapeDtypeStruct((ff, width), BF16),
            jax.ShapeDtypeStruct((total, width), BF16),
            jax.ShapeDtypeStruct((total, tok_rows), BF16),
        ),
        in_specs=[hbm_spec] * 7,
        out_specs=[vmem_spec] * 5,
        scratch_shapes=[
            pltpu.VMEM((width, ff), BF16),
            pltpu.VMEM((width, ff), BF16),
            pltpu.VMEM((ff, width), BF16),
            pltpu.VMEM((top_count, tok_rows), jnp.int32),
            pltpu.VMEM((top_count, tok_rows), F32),
            pltpu.VMEM((n_ep, tok_rows), F32),
            pltpu.VMEM((chunks, n_ep, tok_rows), jnp.int32),
            pltpu.VMEM((chunks, n_ep, tok_rows), F32),
            pltpu.VMEM((chunks, 2, tok_rows, width), BF16),
            pltpu.VMEM((2, total // 2, width), BF16),
            pltpu.VMEM((2, total, width), BF16),
            pltpu.VMEM((chunks, 3, 2 * rows, ff), BF16),
            pltpu.VMEM((chunks, 3, rows, ff), BF16),
            pltpu.VMEM((chunks, 3, rows, ff), BF16),
            pltpu.VMEM((chunks, 3, rows, ff), BF16),
            pltpu.VMEM((3, total, ff), BF16),
            pltpu.VMEM((total, width), BF16),
            pltpu.VMEM((width, total), BF16),
            pltpu.VMEM((ff, total), BF16),
            pltpu.VMEM((total, width), BF16),
            pltpu.VMEM((total, ff), BF16),
            pltpu.VMEM((total, ff), BF16),
            dma((3,)),
            dma((4,)),
            dma((chunks,)),
            dma((chunks,)),
            dma((2, chunks, 2)),
            dma((2, chunks, 2)),
            dma((chunks, 2)),
            dma((chunks, 2)),
            dma((chunks, 2)),
            dma((chunks, 2)),
            dma((chunks, 2)),
            dma((chunks, 2)),
            dma((chunks, 2)),
            dma((chunks, 2)),
            dma((n_ep,)),
            dma((n_ep,)),
        ],
        compiler_params=pltpu.CompilerParams(
            collective_id=0, has_side_effects=True, vmem_limit_bytes=VMEM_BYTES
        ),
    )(*(
        pltpu.with_memory_space_constraint(x, pltpu.HBM)
        for x in (tokens, out_grad, expert_ids.T, route_probs.T, w_gate, w_up, w_down)
    ))
    return pl.pallas_call(
        finish_kernel,
        out_shape=(
            jax.ShapeDtypeStruct(tokens.shape, BF16),
            jax.ShapeDtypeStruct(w_gate.shape, BF16),
            jax.ShapeDtypeStruct(w_up.shape, BF16),
            jax.ShapeDtypeStruct(w_down.shape, BF16),
        ),
        in_specs=[vmem_spec] * 5,
        out_specs=[hbm_spec] * 4,
        scratch_shapes=[pltpu.VMEM(tokens.shape, BF16), dma((4,))],
        compiler_params=pltpu.CompilerParams(vmem_limit_bytes=8 * 1024 * 1024),
    )(*fishers, returned, onehot)


def part(n_ep, n_tp, *args):
    tokens, expert_ids, w_gate = args[0], args[2], args[4]
    width, ff = w_gate.shape[1:]
    rows = slot_rows(tokens.shape[0], expert_ids.shape[1], n_ep)
    fits = (
        n_tp == 4
        and n_ep == 8
        and tokens.shape[0] % LANES == 0
        and ff <= width
        and ff % (2 * LANES) == 0
        and width % LANES == 0
        and n_ep * rows * (17 * width + 22 * ff) + 14 * width * ff < VMEM_BYTES
    )
    if fits:
        return fused_on_device(n_ep, n_tp, *args)
    return on_device(*args)


def solution(mesh):
    in_specs = (
        P("ep", "tp"),
        P("ep", "tp"),
        P("ep", None),
        P("ep", None),
        P("ep", "tp", None),
        P("ep", "tp", None),
        P("ep", None, "tp"),
    )
    out_specs = (P("ep", "tp"), P("ep", "tp", None), P("ep", "tp", None), P("ep", None, "tp"))
    return jax.shard_map(
        functools.partial(part, mesh.shape["ep"], mesh.shape["tp"]), mesh=mesh, in_specs=in_specs, out_specs=out_specs, check_vma=False
    )
```
